128 devices in a mesh: wide: 8 (over x, core), rep: 16 (over y, z).
Axes of the slice: x: 4, y: 4, z: 4, core: 2. Of those that a mesh axis runs over, the one named last changes fastest.
Arguments:
- stretch_qkv: bfloat16 [16, 1536, 3, 5120], P('rep', 'wide'), may hold values from -60 to 60
- norm_gains: float32 [2, 5120], replicated, may hold values from 0.25 to 1.75
- cache: bfloat16 [256, 2, 192, 5120], P('rep', None, 'wide'), may hold values from -6 to 6
- cached_stretches: int32 [16], replicated, may hold values from 1 to 2, as said below
- block_slot: int32 [16, 16], replicated, may hold values from 0 to 255, as said below
- video_of_group: int32 [16], replicated, may hold values from 0 to 15, each once
Outputs:
- attended: bfloat16 [16, 1536, 5120], P('rep', 'wide')
The draws below stay inside these ranges and needn't reach their ends.
Inputs may be any that keep to these rules, and one draw needn't show every extreme that they name: `cached_stretches`: each value is 1 to 2; some video has exactly 2. Block b of video u holds that video's cached tokens b * 192 to (b + 1) * 192 - 1, oldest first; it is cache row block_slot[u, b], owned by group block_slot[u, b] // 16. Every group owns exactly 1 block of every video; no two blocks share a row.
All inputs are finite; a program needn't handle non-finite values.
Results may differ from the reference program's by a relative error of at most 0.011.
Values may be sent and summed in bfloat16 or wider, within the bound.
A program may use at most 128 MiB of HBM per device.

```python
import math
import jax
import jax.numpy as jnp
from jax import lax

D = 5120
HEADS = 40
HD = 128
MAXC = 2
STRETCH = 1536
BLK = 192
NBLK = 16
VIDEOS = 16
CAP = 1
SLOTS = 16
KEYS = 4608
N_REP = 16


def draw_stretch_qkv(key, part):
    subkeys = jax.random.split(key, 3)
    full_shape = (VIDEOS, STRETCH, 3, D)
    draws_base = jax.random.normal(subkeys[0], full_shape, jnp.float32)
    log_ten = math.log(10.0)
    column_scale = jnp.exp(log_ten * jax.random.uniform(subkeys[1], (1, 1, 1, D), jnp.float32))
    row_scale = jnp.exp(log_ten * jax.random.uniform(subkeys[2], (VIDEOS, STRETCH, 1, 1), jnp.float32))
    component = jnp.arange(3).reshape(1, 1, 3, 1)
    scaled = jnp.where(component < 2, draws_base * column_scale * row_scale, draws_base)
    return jnp.clip(scaled, -60.0, 60.0).astype(jnp.bfloat16)


def draw_cached_stretches(key, part):
    counts = jax.random.randint(key, (VIDEOS,), 1, MAXC + 1)
    forced = jax.random.randint(jax.random.fold_in(key, 7), (), 0, VIDEOS)
    return jnp.where(jnp.arange(VIDEOS) == forced, MAXC, counts).astype(jnp.int32)


def draw_block_slot(key, part):
    owner_key = jax.random.fold_in(key, 11)
    slot_key = jax.random.fold_in(key, 12)
    owner_order = jax.vmap(lambda subkey: jax.random.permutation(subkey, VIDEOS))(jax.random.split(owner_key, VIDEOS))
    slot_order = jax.vmap(lambda subkey: jax.random.permutation(subkey, VIDEOS))(jax.random.split(slot_key, VIDEOS))
    block_index = jnp.arange(NBLK)
    owner_group = owner_order[:, block_index % VIDEOS]
    within = (block_index // VIDEOS)[None, :]
    video_index = jnp.arange(VIDEOS)[:, None]
    rank_here = slot_order[owner_group, video_index]
    return (owner_group * SLOTS + rank_here * CAP + within).astype(jnp.int32)


def block_scale(key, extent, cuts, low, largest):
    factor_of = 1.0
    for axis_at, parts in cuts:
        steps = jax.random.uniform(jax.random.fold_in(jax.random.fold_in(key, 6), axis_at), (parts,), jnp.float32, low / len(cuts), largest / len(cuts))
        factor_of = factor_of * jnp.repeat(jnp.exp(steps), extent[axis_at] // parts).reshape((-1,) + (1,) * (len(extent) - 1 - axis_at))
    return factor_of


def bell_draw(own_key, extent, scale, limit, pieces=(), kind=jnp.bfloat16):
    result = jax.random.normal(own_key, extent, jnp.float32) * scale
    if len(pieces) > 0:
        result = block_scale(own_key, extent, pieces, -0.22, 0.18) * result
    return jnp.clip(result, min=-limit, max=limit).astype(kind)


def setup_inputs(seed: int = 0) -> dict:
    splits = jax.random.split(jax.random.key(seed), 7)
    stretch_qkv = draw_stretch_qkv(jax.random.fold_in(splits[6], 71), 0)
    norm_gains = jnp.clip(1.0 + 0.15 * jax.random.normal(splits[1], (2, D), jnp.float32), 0.25, 1.75)
    cache = bell_draw(splits[2], (N_REP * SLOTS, 2, BLK, D), 1.0, 6.0, ((0, 16), (2, 8)))
    cached_stretches = draw_cached_stretches(jax.random.fold_in(splits[6], 71), 0)
    block_slot = draw_block_slot(jax.random.fold_in(splits[6], 71), 0)
    video_of_group = jax.random.permutation(splits[5], VIDEOS).astype(jnp.int32)
    return {"stretch_qkv": stretch_qkv, "norm_gains": norm_gains, "cache": cache, "cached_stretches": cached_stretches, "block_slot": block_slot, "video_of_group": video_of_group}


epsilon = 1e-06

def normalize(stretch_rows, gains_row):
    widened = stretch_rows.astype(jnp.float32)
    mean_square = lax.optimization_barrier(jnp.mean(widened * widened, axis=-1, keepdims=True))
    return (widened * lax.rsqrt(mean_square + epsilon) * gains_row).astype(jnp.bfloat16)

def attend_block(query_rows, all_keys, all_values, usable):
    scores = jnp.einsum('qhd,khd->hqk', query_rows.astype(jnp.float32), all_keys.astype(jnp.float32)) * HD ** (-0.5)
    scores = jnp.where(usable[None, None, :], scores, -jnp.inf)
    row_max = lax.optimization_barrier(jnp.max(scores, axis=-1, keepdims=True))
    weights = jnp.exp(scores - row_max)
    row_total = lax.optimization_barrier(jnp.sum(weights, axis=-1, keepdims=True))
    rounded = lax.optimization_barrier(weights.astype(jnp.bfloat16)).astype(jnp.float32)
    mixed = jnp.einsum('hqk,khd->qhd', rounded, all_values.astype(jnp.float32))
    return (mixed / jnp.transpose(row_total, (1, 0, 2))).astype(jnp.bfloat16)

def reference(stretch_qkv, norm_gains, cache, cached_stretches, block_slot, video_of_group):
    query_block = math.gcd(STRETCH, 256)

    def one_group(group_index):
        own_video = video_of_group[group_index]
        stretch_rows = stretch_qkv[group_index]
        queries = normalize(stretch_rows[:, 0], norm_gains[0])
        keys_new = normalize(stretch_rows[:, 1], norm_gains[1])
        held_blocks = cache[block_slot[own_video]]
        all_keys = jnp.concatenate([held_blocks[:, 0].reshape(NBLK * BLK, D), keys_new], axis=0)
        all_values = jnp.concatenate([held_blocks[:, 1].reshape(NBLK * BLK, D), stretch_rows[:, 2]], axis=0)
        all_keys = all_keys.reshape(KEYS, HEADS, HD)
        all_values = all_values.reshape(KEYS, HEADS, HD)
        key_position = jnp.arange(KEYS, dtype=jnp.int32)
        usable = (key_position < cached_stretches[own_video] * STRETCH) | (key_position >= NBLK * BLK)
        blocks_q = queries.reshape(STRETCH // query_block, query_block, HEADS, HD)
        attended = lax.map(lambda piece: attend_block(piece, all_keys, all_values, usable), blocks_q)
        return attended.reshape(STRETCH, D)
    return lax.map(one_group, jnp.arange(VIDEOS, dtype=jnp.int32))
```

```python
import functools
import math

import jax
import jax.numpy as jnp
from jax import lax
from jax.experimental import pallas as pl
from jax.experimental.pallas import tpu as pltpu
from jax.sharding import PartitionSpec as P

MESH = pl.DeviceIdType.MESH
HD = 128
HEADS_CHUNK = 4
SLOTS = 3
CHUNK = HD * HEADS_CHUNK
EPSILON = 1e-06
SCALE = math.log2(math.e) / math.sqrt(HD)
ORDER = ((1, 0), (0, 1), (3, 2), (2, 3), (3, 0), (0, 3), (1, 2), (2, 1), (2, 0), (0, 2), (1, 1), (3, 3), (1, 3), (3, 1), (2, 2))


def lanes(start, size):
    return pl.ds(pl.multiple_of(start, 128), size)


def kernel(
    sel_ref, vis_ref, qkv_ref, gains_ref, cache_ref, out_ref,
    qk, raw_even, raw_odd, gathered, arrived, queries, keys_new, values_new, keys, values, partial, relay_in, final_in,
    stats_col, stats, relay_stats, final_stats, weights_row,
    load_sem, raw_sem, own_sem, cache_send, cache_recv, first_send, first_recv, hop_send, hop_recv,
    kv_send, kv_recv, s1_send, s1_recv, s2_send, s2_recv, out_send, out_recv, out_own,
):
    wide, rep = lax.axis_index("wide"), lax.axis_index("rep")
    x, core = wide // 2, wide % 2
    y, z = rep // 4, rep % 4
    other = 1 - core
    right, left = (x + 1) % 4, (x + 3) % 4
    chunks, rows_all, _ = queries.shape
    tokens = qk.shape[1]
    quarter = 2 * tokens
    half_width = chunks * CHUNK
    groups = sel_ref.shape[0]
    raws = (raw_even, raw_odd)

    def remote(src, dst, send, recv, to_wide, to_rep):
        return pltpu.make_async_remote_copy(
            src_ref=src, dst_ref=dst, send_sem=send, recv_sem=recv, device_id=(to_wide, to_rep), device_id_type=MESH
        )

    def group_at(k):
        dy, dz = ORDER[k]
        sign = 1 - 2 * core
        return ((y + dy * sign + 4) % 4) * 4 + (z + dz * sign + 4) % 4

    def cache_copies(j):
        copies = []
        for k in range(len(ORDER)):
            to = group_at(k)
            for h in range(2):
                copies.append(remote(
                    gathered.at[j % SLOTS, to, h], arrived.at[j, rep, core], cache_send.at[j, 2 * k + h],
                    cache_recv.at[j, rep * 2 + core], 2 * x + h, to))
        copies.append(remote(
            gathered.at[j % SLOTS, rep, other], arrived.at[j, rep, core], cache_send.at[j, 2 * len(ORDER)],
            cache_recv.at[j, rep * 2 + core], 2 * x + other, rep))
        return copies

    def wait_cache(j):
        for k in range(len(ORDER)):
            owner = group_at(k)
            for h in range(2):
                remote(gathered.at[0, 0, 0], arrived.at[j, owner, h], cache_send.at[j, 0],
                       cache_recv.at[j, owner * 2 + h], wide, rep).wait_recv()
        remote(gathered.at[0, 0, 0], arrived.at[j, rep, other], cache_send.at[j, 0],
               cache_recv.at[j, rep * 2 + other], wide, rep).wait_recv()

    def piece(j, position):
        return queries.at[j, pl.ds(pl.multiple_of(position * tokens, 16), tokens)]

    def own_columns(h, j):
        return lanes(h * half_width + j * CHUNK, CHUNK)

    def first_copies(j):
        copies = [remote(qk.at[0, :, own_columns(other, j)], piece(j, wide), first_send.at[j, 0], first_recv.at[j, 0],
                         2 * x + other, rep)]
        for side, to in enumerate((right, left)):
            for h in range(2):
                copies.append(remote(
                    qk.at[0, :, own_columns(h, j)], piece(j, wide), first_send.at[j, 1 + 2 * side + h],
                    first_recv.at[j, 1 + 2 * side + core], 2 * to + h, rep))
        return copies

    def wait_first(j):
        sources = [2 * x + other, 2 * left, 2 * left + 1, 2 * right, 2 * right + 1]
        for slot, source in enumerate(sources):
            remote(piece(j, wide), piece(j, source), first_send.at[j, 0], first_recv.at[j, slot], wide, rep).wait_recv()

    def hop_copies(j):
        return [
            remote(piece(j, 2 * left), piece(j, 2 * left), hop_send.at[j, 0], hop_recv.at[j, 0], 2 * right + core, rep),
            remote(piece(j, 2 * right + 1), piece(j, 2 * right + 1), hop_send.at[j, 1], hop_recv.at[j, 1], 2 * left + core, rep),
        ]

    def wait_hop(j):
        far = (x + 2) % 4
        for slot in range(2):
            remote(piece(j, wide), piece(j, 2 * far + slot), hop_send.at[j, 0], hop_recv.at[j, slot], wide, rep).wait_recv()

    def token_rows(c):
        return pl.ds(pl.multiple_of(c * tokens, 16), tokens)

    def kv_copies(j):
        return [
            remote(qk.at[1, :, own_columns(other, j)], keys_new.at[j, token_rows(core)], kv_send.at[j, 0], kv_recv.at[j, 0],
                   2 * x + other, rep),
            remote(qkv_ref.at[2, :, own_columns(other, j)], values_new.at[j, token_rows(core)], kv_send.at[j, 1],
                   kv_recv.at[j, 1], 2 * x + other, rep),
        ]

    def wait_kv(j):
        remote(keys_new.at[j, token_rows(core)], keys_new.at[j, token_rows(other)], kv_send.at[j, 0], kv_recv.at[j, 0],
               wide, rep).wait_recv()
        remote(keys_new.at[j, token_rows(core)], values_new.at[j, token_rows(other)], kv_send.at[j, 1], kv_recv.at[j, 1],
               wide, rep).wait_recv()

    def own_copies(j):
        return [
            pltpu.make_async_copy(qk.at[0, :, own_columns(core, j)], piece(j, wide), own_sem.at[j, 0]),
            pltpu.make_async_copy(qk.at[1, :, own_columns(core, j)], keys_new.at[j, token_rows(core)], own_sem.at[j, 1]),
            pltpu.make_async_copy(qkv_ref.at[2, :, own_columns(core, j)], values_new.at[j, token_rows(core)], own_sem.at[j, 2]),
        ]

    def raw_copies(j):
        return [
            pltpu.make_async_copy(cache_ref.at[:, :, :, :, own_columns(h, j)], raws[j % 2].at[h], raw_sem.at[j % 2, h])
            for h in range(2)
        ]

    def gather(j):
        for copy in raw_copies(j):
            copy.wait()

        def place(to, carry):
            row = sel_ref[to]
            for h in range(2):
                gathered[j % SLOTS, to, h] = raws[j % 2][h, row]
            return carry

        lax.fori_loop(0, groups, place, 0)
        arrived[j, rep, core] = raws[j % 2][core, sel_ref[rep]]

        if j + 2 < chunks:
            start(raw_copies(j + 2))

    def normalize(which):
        def rows_step(i, carry):
            block = pl.ds(pl.multiple_of(i * 16, 16), 16)
            widened = qk[which, block, :].astype(jnp.float32)
            mean_square = jnp.mean(widened * widened, axis=-1, keepdims=True)
            scaled = widened * lax.rsqrt(mean_square + EPSILON) * gains_ref[which : which + 1, :]
            qk[which, block, :] = scaled.astype(jnp.bfloat16)
            return carry

        lax.fori_loop(0, tokens // 16, rows_step, 0)

    def start(copies):
        for copy in copies:
            copy.start()

    def quarter_rows(d):
        return pl.ds(pl.multiple_of(d * quarter, 16), quarter)

    def half_rows(d, part):
        return pl.ds(pl.multiple_of(d * quarter + part * tokens, 16), tokens)

    def s1_copies(j):
        far = (x + 2) % 4
        copies = []
        for slot, to in enumerate((right, left)):
            copies.append(remote(partial.at[j, half_rows(far, 1 - slot)], relay_in.at[j, slot], s1_send.at[j, 2 * slot],
                                 s1_recv.at[j, 2 * slot], 2 * to + core, rep))
            copies.append(remote(stats.at[j, far], relay_stats.at[j, slot], s1_send.at[j, 2 * slot + 1],
                                 s1_recv.at[j, 2 * slot + 1], 2 * to + core, rep))
        return copies

    def s2_copies(j, slot):
        to = (right, left)[slot]
        return [
            remote(partial.at[j, quarter_rows(to)], final_in.at[j, slot], s2_send.at[j, 2 * slot], s2_recv.at[j, 2 * slot],
                   2 * to + core, rep),
            remote(stats.at[j, to], final_stats.at[j, slot], s2_send.at[j, 2 * slot + 1], s2_recv.at[j, 2 * slot + 1],
                   2 * to + core, rep),
        ]

    def forward_partial(j):
        for slot, to in enumerate((right, left)):
            remote(relay_in.at[j, slot], relay_in.at[j, slot], s1_send.at[j, 0], s1_recv.at[j, 2 * slot], wide, rep).wait_recv()
            remote(relay_stats.at[j, slot], relay_stats.at[j, slot], s1_send.at[j, 0], s1_recv.at[j, 2 * slot + 1], wide,
                   rep).wait_recv()
            here, came = stats[j, to], relay_stats[j, slot]
            top = jnp.maximum(here, came)
            a, b = jnp.exp2(here - top), jnp.exp2(came - top)
            total = a + b
            token = lax.broadcasted_iota(jnp.int32, here.shape, 1)
            merged = token >= tokens if slot == 0 else token < tokens
            stats[j, to] = jnp.where(merged, top + jnp.log2(total), here)
            weights_row[0:8] = a / total
            weights_row[8:16] = b / total
            part = 1 - slot
            columns = jnp.transpose(weights_row[...])[part * tokens : (part + 1) * tokens]
            place = half_rows(to, part)
            for h in range(HEADS_CHUNK):
                feature = slice(h * HD, (h + 1) * HD)
                mixed = columns[:, h : h + 1] * partial[j, place, feature].astype(jnp.float32)
                mixed += columns[:, 8 + h : 9 + h] * relay_in[j, slot, :, feature].astype(jnp.float32)
                partial[j, place, feature] = mixed.astype(jnp.bfloat16)
            start(s2_copies(j, slot))

    def out_copies(j):
        place = own_columns(core, j)
        return (
            remote(partial.at[j, half_rows(x, other)], out_ref.at[:, place], out_send.at[j], out_recv.at[j], 2 * x + other, rep),
            pltpu.make_async_copy(partial.at[j, half_rows(x, core)], out_ref.at[:, place], out_own.at[j]),
        )

    def finish(j):
        for slot in range(2):
            remote(final_in.at[j, slot], final_in.at[j, slot], s2_send.at[j, 0], s2_recv.at[j, 2 * slot], wide, rep).wait_recv()
            remote(final_stats.at[j, slot], final_stats.at[j, slot], s2_send.at[j, 0], s2_recv.at[j, 2 * slot + 1], wide,
                   rep).wait_recv()
        here, first, second = stats[j, x], final_stats[j, 0], final_stats[j, 1]
        top = jnp.maximum(here, jnp.maximum(first, second))
        a, b, c = jnp.exp2(here - top), jnp.exp2(first - top), jnp.exp2(second - top)
        total = a + b + c
        weights_row[0:8] = a / total
        weights_row[8:16] = b / total
        weights_row[16:24] = c / total
        columns = jnp.transpose(weights_row[...])
        place = quarter_rows(x)
        for h in range(HEADS_CHUNK):
            feature = slice(h * HD, (h + 1) * HD)
            mixed = columns[:, h : h + 1] * partial[j, place, feature].astype(jnp.float32)
            mixed += columns[:, 8 + h : 9 + h] * final_in[j, 0, :, feature].astype(jnp.float32)
            mixed += columns[:, 16 + h : 17 + h] * final_in[j, 1, :, feature].astype(jnp.float32)
            partial[j, place, feature] = mixed.astype(jnp.bfloat16)
        start(out_copies(j))

    def prepare(j):
        keys[0:quarter] = keys_new[j]
        for h in range(HEADS_CHUNK):
            values[h, 0:quarter, 0:HD] = values_new[j, :, h * HD : (h + 1) * HD]
        rows = quarter // 8

        def block(owner, carry):
            seen = vis_ref[owner]
            count = 2 * 24
            here = pl.ds(pl.multiple_of(quarter + owner * count, 16), count)
            spare = keys_new[j, 0:count].astype(jnp.float32)
            k = arrived[j, owner, :, 0].astype(jnp.float32).reshape(count, CHUNK)
            v = arrived[j, owner, :, 1].astype(jnp.float32).reshape(count, CHUNK)
            keys[here] = (k * seen + spare * (1.0 - seen)).astype(jnp.bfloat16)
            v = (v * seen).astype(jnp.bfloat16)
            for h in range(HEADS_CHUNK):
                values[h, here, 0:HD] = v[:, h * HD : (h + 1) * HD]
            return carry

        lax.fori_loop(0, groups, block, 0)

    def attend(j, h):
        feature = lanes(h * HD, HD)
        tile = rows_all // 2
        k = keys[:, feature]
        lane = lax.broadcasted_iota(jnp.int32, (tile, 128), 1)
        for part in range(2):
            place = slice(part * tile, (part + 1) * tile)
            q = queries[j, place, feature]
            scores = lax.dot_general(q, k, (((1,), (1,)), ((), ())), preferred_element_type=jnp.float32)
            row_max = jnp.max(scores, axis=1, keepdims=True) * SCALE
            weights = jnp.exp2(scores * SCALE - row_max)
            mixed = jnp.dot(weights.astype(jnp.bfloat16), values[h], preferred_element_type=jnp.float32)
            total = mixed[:, HD:]
            partial[j, place, feature] = (mixed[:, :HD] / total).astype(jnp.bfloat16)
            stats_col[place, :] = jnp.where(lane == h, row_max + jnp.log2(total), stats_col[place, :])

    barrier = pltpu.get_barrier_semaphore()
    peers = [(2 * x + h, group_at(k)) for k in range(len(ORDER)) for h in range(2)]
    peers += [(2 * x + other, rep)] + [(2 * to + h, rep) for to in (right, left) for h in range(2)]
    for peer in peers:
        pl.semaphore_signal(barrier, inc=1, device_id=peer, device_id_type=MESH)
    loads = [pltpu.make_async_copy(qkv_ref.at[i], qk.at[i], load_sem.at[i]) for i in range(2)]
    loads[0].start()
    start(raw_copies(0))
    loads[1].start()
    start(raw_copies(1))
    for h in range(HEADS_CHUNK):
        values[h, 0:quarter, HD:] = jnp.ones((quarter, HD), jnp.bfloat16)

    def shares(owner, carry):
        count = 2 * 24
        here = pl.ds(pl.multiple_of(quarter + owner * count, 16), count)
        filled = jnp.full((count, HD), vis_ref[owner], jnp.float32).astype(jnp.bfloat16)
        for h in range(HEADS_CHUNK):
            values[h, here, HD:] = filled
        return carry

    lax.fori_loop(0, groups, shares, 0)
    stats_col[...] = jnp.zeros_like(stats_col)
    weights_row[...] = jnp.zeros_like(weights_row)
    gather(0)
    loads[0].wait()
    normalize(0)
    pl.semaphore_wait(barrier, len(peers))
    start(cache_copies(0))
    start(first_copies(0))
    gather(1)
    start(cache_copies(1))
    start(first_copies(1))
    loads[1].wait()
    normalize(1)

    def spread(j, carry):
        start(own_copies(j))
        start(kv_copies(j))
        return carry

    lax.fori_loop(0, chunks, spread, 0)

    for j in range(2, SLOTS):
        gather(j)
        start(cache_copies(j))
    wait_first(0)
    start(hop_copies(0))
    start(first_copies(2))

    def step(j, carry):
        @pl.when(j >= 1)
        def _():
            forward_partial(j - 1)

        wait_hop(j)
        wait_kv(j)
        for copy in own_copies(j):
            copy.wait()
        wait_cache(j)
        prepare(j)
        attend(j, 0)

        @pl.when(j + 1 < chunks)
        def _():
            wait_first(j + 1)
            start(hop_copies(j + 1))

        @pl.when(j + 3 < chunks)
        def _():
            start(first_copies(j + 3))

        for early in range(chunks - SLOTS):

            @pl.when(j == early)
            def _():
                for copy in cache_copies(early):
                    copy.wait_send()
                gather(early + SLOTS)
                start(cache_copies(early + SLOTS))

        def rest(h, inner):
            attend(j, h)
            return inner

        lax.fori_loop(1, HEADS_CHUNK, rest, 0)
        for d in range(4):
            stats[j, d] = jnp.transpose(stats_col[d * quarter : (d + 1) * quarter, :])[0:8]
        start(s1_copies(j))

        @pl.when(j >= 1)
        def _():
            finish(j - 1)

        return carry

    lax.fori_loop(0, chunks, step, 0)
    forward_partial(chunks - 1)
    finish(chunks - 1)

    def drain(j, carry):
        @pl.when(j + SLOTS >= chunks)
        def _():
            for copy in cache_copies(j):
                copy.wait_send()

        for copy in first_copies(j) + hop_copies(j) + kv_copies(j) + s1_copies(j) + s2_copies(j, 0) + s2_copies(j, 1):
            copy.wait_send()
        sent, kept = out_copies(j)
        sent.wait_send()
        sent.wait_recv()
        kept.wait()
        return carry

    lax.fori_loop(0, chunks, drain, 0)


def body(stretch_qkv, norm_gains, cache, cached_stretches, block_slot, video_of_group):
    rep = lax.axis_index("rep")
    groups = lax.axis_size("rep")
    _, tokens, _, width = stretch_qkv.shape
    slots = cache.shape[0]
    blocks = block_slot.shape[1]
    stretch = tokens * lax.axis_size("wide")
    block_len = cache.shape[2] * lax.axis_size("wide")
    videos = cached_stretches.shape[0]
    chunks = width // 2 // CHUNK
    picked = video_of_group[:, None] == jnp.arange(videos, dtype=jnp.int32)[None, :]
    table = jnp.sum(jnp.where(picked[:, :, None], block_slot[None], 0), axis=1)
    sel = jnp.sum(jnp.where(table // slots == rep, table % slots, 0), axis=1)
    mine = jnp.arange(groups, dtype=jnp.int32) == rep
    own_table = jnp.sum(jnp.where(mine[:, None], table, 0), axis=0)
    own_count = jnp.sum(jnp.where(mine[:, None] & picked, cached_stretches[None, :], 0))
    seen = jnp.arange(blocks, dtype=jnp.int32) * block_len < own_count * stretch
    from_owner = own_table[None, :] // slots == jnp.arange(groups, dtype=jnp.int32)[:, None]
    vis = jnp.sum(jnp.where(from_owner & seen[None, :], 1.0, 0.0), axis=1)

    bf16, f32 = jnp.bfloat16, jnp.float32
    rows_all = stretch
    quarter = 2 * tokens
    keys_count = quarter + groups * 2 * cache.shape[2]
    vmem, dma = pltpu.VMEM, pltpu.SemaphoreType.DMA
    peers = 2 * len(ORDER) + 1
    smem_spec = pl.BlockSpec(memory_space=pltpu.SMEM)
    any_spec = pl.BlockSpec(memory_space=pl.ANY)
    out = pl.pallas_call(
        kernel,
        name="attend_exchange",
        out_shape=jax.ShapeDtypeStruct((tokens, width), bf16),
        in_specs=[smem_spec, smem_spec, any_spec, pl.BlockSpec(memory_space=vmem), any_spec],
        out_specs=any_spec,
        scratch_shapes=[
            vmem((2, tokens, width), bf16),
            vmem((2, slots, 2, 3, 8, CHUNK), bf16),
            vmem((2, slots, 2, 3, 8, CHUNK), bf16),
            vmem((SLOTS, groups, 2, 2, 3, 8, CHUNK), bf16),
            vmem((chunks, groups, 2, 2, 3, 8, CHUNK), bf16),
            vmem((chunks, rows_all, CHUNK), bf16),
            vmem((chunks, quarter, CHUNK), bf16),
            vmem((chunks, quarter, CHUNK), bf16),
            vmem((keys_count, CHUNK), bf16),
            vmem((HEADS_CHUNK, keys_count, 2 * HD), bf16),
            vmem((chunks, rows_all, CHUNK), bf16),
            vmem((chunks, 2, tokens, CHUNK), bf16),
            vmem((chunks, 2, quarter, CHUNK), bf16),
            vmem((rows_all, 128), f32),
            vmem((chunks, 4, 8, quarter), f32),
            vmem((chunks, 2, 8, quarter), f32),
            vmem((chunks, 2, 8, quarter), f32),
            vmem((128, quarter), f32),
            dma((2,)),
            dma((2, 2)),
            dma((chunks, 3)),
            dma((chunks, peers)),
            dma((chunks, 2 * groups)),
            dma((chunks, 5)),
            dma((chunks, 5)),
            dma((chunks, 2)),
            dma((chunks, 2)),
            dma((chunks, 2)),
            dma((chunks, 2)),
            dma((chunks, 4)),
            dma((chunks, 4)),
            dma((chunks, 4)),
            dma((chunks, 4)),
            dma((chunks,)),
            dma((chunks,)),
            dma((chunks,)),
        ],
        compiler_params=pltpu.CompilerParams(collective_id=0, has_side_effects=True, vmem_limit_bytes=67043328),
    )(sel, vis, jnp.transpose(stretch_qkv[0], (1, 0, 2)), norm_gains, cache.reshape(slots, 2, 3, 8, width))
    return out[None]


def solution(mesh):
    in_specs = (P("rep", "wide", None, None), P(), P("rep", None, "wide", None), P(), P(), P())
    out_specs = P("rep", "wide", None)
    return jax.shard_map(body, mesh=mesh, in_specs=in_specs, out_specs=out_specs, check_vma=False)
```

```python
import functools
import math

import jax
import jax.numpy as jnp
from jax import lax
from jax.experimental import pallas as pl
from jax.experimental.pallas import tpu as pltpu
from jax.sharding import PartitionSpec as P

MESH = pl.DeviceIdType.MESH
HD = 128
HEADS_CHUNK = 4
SLOTS = 3
CHUNK = HD * HEADS_CHUNK
EPSILON = 1e-06
SCALE = math.log2(math.e) / math.sqrt(HD)
ORDER = ((1, 0), (0, 1), (3, 2), (2, 3), (3, 0), (0, 3), (1, 2), (2, 1), (2, 0), (0, 2), (1, 1), (3, 3), (1, 3), (3, 1), (2, 2))


def lanes(start, size):
    return pl.ds(pl.multiple_of(start, 128), size)


def kernel(
    counts_ref, slot_ref, video_ref, qkv_ref, gains_ref, cache_ref, out_ref,
    qk, raw_even, raw_odd, gathered, arrived, queries, keys_new, values_new, keys, values, partial, relay_in, final_in,
    stats_col, stats, relay_stats, final_stats, weights_row, sel_ref, vis_ref,
    load_sem, raw_sem, own_sem, cache_send, cache_recv, first_send, first_recv, hop_send, hop_recv,
    kv_send, kv_recv, s1_send, s1_recv, s2_send, s2_recv, out_send, out_recv, out_own,
):
    wide, rep = lax.axis_index("wide"), lax.axis_index("rep")
    x, core = wide // 2, wide % 2
    y, z = rep // 4, rep % 4
    other = 1 - core
    right, left = (x + 1) % 4, (x + 3) % 4
    chunks, rows_all, _ = queries.shape
    tokens = qk.shape[1]
    quarter = 2 * tokens
    half_width = chunks * CHUNK
    groups, blocks = slot_ref.shape
    rows_held = cache_ref.shape[0]
    raws = (raw_even, raw_odd)

    def remote(src, dst, send, recv, to_wide, to_rep):
        return pltpu.make_async_remote_copy(
            src_ref=src, dst_ref=dst, send_sem=send, recv_sem=recv, device_id=(to_wide, to_rep), device_id_type=MESH
        )

    def group_at(k):
        dy, dz = ORDER[k]
        sign = 1 - 2 * core
        return ((y + dy * sign + 4) % 4) * 4 + (z + dz * sign + 4) % 4

    def cache_copies(j):
        copies = []
        for k in range(len(ORDER)):
            to = group_at(k)
            for h in range(2):
                copies.append(remote(
                    gathered.at[j % SLOTS, to, h], arrived.at[j, rep, core], cache_send.at[j, 2 * k + h],
                    cache_recv.at[j, rep * 2 + core], 2 * x + h, to))
        copies.append(remote(
            gathered.at[j % SLOTS, rep, other], arrived.at[j, rep, core], cache_send.at[j, 2 * len(ORDER)],
            cache_recv.at[j, rep * 2 + core], 2 * x + other, rep))
        return copies

    def wait_cache(j):
        for k in range(len(ORDER)):
            owner = group_at(k)
            for h in range(2):
                remote(gathered.at[0, 0, 0], arrived.at[j, owner, h], cache_send.at[j, 0],
                       cache_recv.at[j, owner * 2 + h], wide, rep).wait_recv()
        remote(gathered.at[0, 0, 0], arrived.at[j, rep, other], cache_send.at[j, 0],
               cache_recv.at[j, rep * 2 + other], wide, rep).wait_recv()

    def piece(j, position):
        return queries.at[j, pl.ds(pl.multiple_of(position * tokens, 16), tokens)]

    def own_columns(h, j):
        return lanes(h * half_width + j * CHUNK, CHUNK)

    def first_copies(j):
        copies = [remote(qk.at[0, :, own_columns(other, j)], piece(j, wide), first_send.at[j, 0], first_recv.at[j, 0],
                         2 * x + other, rep)]
        for side, to in enumerate((right, left)):
            for h in range(2):
                copies.append(remote(
                    qk.at[0, :, own_columns(h, j)], piece(j, wide), first_send.at[j, 1 + 2 * side + h],
                    first_recv.at[j, 1 + 2 * side + core], 2 * to + h, rep))
        return copies

    def wait_first(j):
        sources = [2 * x + other, 2 * left, 2 * left + 1, 2 * right, 2 * right + 1]
        for slot, source in enumerate(sources):
            remote(piece(j, wide), piece(j, source), first_send.at[j, 0], first_recv.at[j, slot], wide, rep).wait_recv()

    def hop_copies(j):
        return [
            remote(piece(j, 2 * left), piece(j, 2 * left), hop_send.at[j, 0], hop_recv.at[j, 0], 2 * right + core, rep),
            remote(piece(j, 2 * right + 1), piece(j, 2 * right + 1), hop_send.at[j, 1], hop_recv.at[j, 1], 2 * left + core, rep),
        ]

    def wait_hop(j):
        far = (x + 2) % 4
        for slot in range(2):
            remote(piece(j, wide), piece(j, 2 * far + slot), hop_send.at[j, 0], hop_recv.at[j, slot], wide, rep).wait_recv()

    def token_rows(c):
        return pl.ds(pl.multiple_of(c * tokens, 16), tokens)

    def kv_copies(j):
        return [
            remote(qk.at[1, :, own_columns(other, j)], keys_new.at[j, token_rows(core)], kv_send.at[j, 0], kv_recv.at[j, 0],
                   2 * x + other, rep),
            remote(qkv_ref.at[2, :, own_columns(other, j)], values_new.at[j, token_rows(core)], kv_send.at[j, 1],
                   kv_recv.at[j, 1], 2 * x + other, rep),
        ]

    def wait_kv(j):
        remote(keys_new.at[j, token_rows(core)], keys_new.at[j, token_rows(other)], kv_send.at[j, 0], kv_recv.at[j, 0],
               wide, rep).wait_recv()
        remote(keys_new.at[j, token_rows(core)], values_new.at[j, token_rows(other)], kv_send.at[j, 1], kv_recv.at[j, 1],
               wide, rep).wait_recv()

    def own_copies(j):
        return [
            pltpu.make_async_copy(qk.at[0, :, own_columns(core, j)], piece(j, wide), own_sem.at[j, 0]),
            pltpu.make_async_copy(qk.at[1, :, own_columns(core, j)], keys_new.at[j, token_rows(core)], own_sem.at[j, 1]),
            pltpu.make_async_copy(qkv_ref.at[2, :, own_columns(core, j)], values_new.at[j, token_rows(core)], own_sem.at[j, 2]),
        ]

    def raw_copies(j):
        return [
            pltpu.make_async_copy(cache_ref.at[:, :, :, :, own_columns(h, j)], raws[j % 2].at[h], raw_sem.at[j % 2, h])
            for h in range(2)
        ]

    def gather(j):
        for copy in raw_copies(j):
            copy.wait()

        def place(to, carry):
            row = sel_ref[to]
            for h in range(2):
                gathered[j % SLOTS, to, h] = raws[j % 2][h, row]
            return carry

        lax.fori_loop(0, groups, place, 0)
        arrived[j, rep, core] = raws[j % 2][core, sel_ref[rep]]

        if j + 2 < chunks:
            start(raw_copies(j + 2))

    def normalize(which):
        def rows_step(i, carry):
            block = pl.ds(pl.multiple_of(i * 16, 16), 16)
            widened = qk[which, block, :].astype(jnp.float32)
            mean_square = jnp.mean(widened * widened, axis=-1, keepdims=True)
            scaled = widened * lax.rsqrt(mean_square + EPSILON) * gains_ref[which : which + 1, :]
            qk[which, block, :] = scaled.astype(jnp.bfloat16)
            return carry

        lax.fori_loop(0, tokens // 16, rows_step, 0)

    def start(copies):
        for copy in copies:
            copy.start()

    def quarter_rows(d):
        return pl.ds(pl.multiple_of(d * quarter, 16), quarter)

    def half_rows(d, part):
        return pl.ds(pl.multiple_of(d * quarter + part * tokens, 16), tokens)

    def s1_copies(j):
        far = (x + 2) % 4
        copies = []
        for slot, to in enumerate((right, left)):
            copies.append(remote(partial.at[j, half_rows(far, 1 - slot)], relay_in.at[j, slot], s1_send.at[j, 2 * slot],
                                 s1_recv.at[j, 2 * slot], 2 * to + core, rep))
            copies.append(remote(stats.at[j, far], relay_stats.at[j, slot], s1_send.at[j, 2 * slot + 1],
                                 s1_recv.at[j, 2 * slot + 1], 2 * to + core, rep))
        return copies

    def s2_copies(j, slot):
        to = (right, left)[slot]
        return [
            remote(partial.at[j, quarter_rows(to)], final_in.at[j, slot], s2_send.at[j, 2 * slot], s2_recv.at[j, 2 * slot],
                   2 * to + core, rep),
            remote(stats.at[j, to], final_stats.at[j, slot], s2_send.at[j, 2 * slot + 1], s2_recv.at[j, 2 * slot + 1],
                   2 * to + core, rep),
        ]

    def forward_partial(j):
        for slot, to in enumerate((right, left)):
            remote(relay_in.at[j, slot], relay_in.at[j, slot], s1_send.at[j, 0], s1_recv.at[j, 2 * slot], wide, rep).wait_recv()
            remote(relay_stats.at[j, slot], relay_stats.at[j, slot], s1_send.at[j, 0], s1_recv.at[j, 2 * slot + 1], wide,
                   rep).wait_recv()
            here, came = stats[j, to], relay_stats[j, slot]
            top = jnp.maximum(here, came)
            a, b = jnp.exp2(here - top), jnp.exp2(came - top)
            total = a + b
            token = lax.broadcasted_iota(jnp.int32, here.shape, 1)
            merged = token >= tokens if slot == 0 else token < tokens
            stats[j, to] = jnp.where(merged, top + jnp.log2(total), here)
            weights_row[0:8] = a / total
            weights_row[8:16] = b / total
            part = 1 - slot
            columns = jnp.transpose(weights_row[...])[part * tokens : (part + 1) * tokens]
            place = half_rows(to, part)
            for h in range(HEADS_CHUNK):
                feature = slice(h * HD, (h + 1) * HD)
                mixed = columns[:, h : h + 1] * partial[j, place, feature].astype(jnp.float32)
                mixed += columns[:, 8 + h : 9 + h] * relay_in[j, slot, :, feature].astype(jnp.float32)
                partial[j, place, feature] = mixed.astype(jnp.bfloat16)
            start(s2_copies(j, slot))

    def out_copies(j):
        place = own_columns(core, j)
        return (
            remote(partial.at[j, half_rows(x, other)], out_ref.at[:, place], out_send.at[j], out_recv.at[j], 2 * x + other, rep),
            pltpu.make_async_copy(partial.at[j, half_rows(x, core)], out_ref.at[:, place], out_own.at[j]),
        )

    def finish(j):
        for slot in range(2):
            remote(final_in.at[j, slot], final_in.at[j, slot], s2_send.at[j, 0], s2_recv.at[j, 2 * slot], wide, rep).wait_recv()
            remote(final_stats.at[j, slot], final_stats.at[j, slot], s2_send.at[j, 0], s2_recv.at[j, 2 * slot + 1], wide,
                   rep).wait_recv()
        here, first, second = stats[j, x], final_stats[j, 0], final_stats[j, 1]
        top = jnp.maximum(here, jnp.maximum(first, second))
        a, b, c = jnp.exp2(here - top), jnp.exp2(first - top), jnp.exp2(second - top)
        total = a + b + c
        weights_row[0:8] = a / total
        weights_row[8:16] = b / total
        weights_row[16:24] = c / total
        columns = jnp.transpose(weights_row[...])
        place = quarter_rows(x)
        for h in range(HEADS_CHUNK):
            feature = slice(h * HD, (h + 1) * HD)
            mixed = columns[:, h : h + 1] * partial[j, place, feature].astype(jnp.float32)
            mixed += columns[:, 8 + h : 9 + h] * final_in[j, 0, :, feature].astype(jnp.float32)
            mixed += columns[:, 16 + h : 17 + h] * final_in[j, 1, :, feature].astype(jnp.float32)
            partial[j, place, feature] = mixed.astype(jnp.bfloat16)
        start(out_copies(j))

    def prepare(j):
        keys[0:quarter] = keys_new[j]
        for h in range(HEADS_CHUNK):
            values[h, 0:quarter, 0:HD] = values_new[j, :, h * HD : (h + 1) * HD]
        rows = quarter // 8

        def block(owner, carry):
            seen = vis_ref[owner]
            count = 2 * 24
            here = pl.ds(pl.multiple_of(quarter + owner * count, 16), count)
            spare = keys_new[j, 0:count].astype(jnp.float32)
            k = arrived[j, owner, :, 0].astype(jnp.float32).reshape(count, CHUNK)
            v = arrived[j, owner, :, 1].astype(jnp.float32).reshape(count, CHUNK)
            keys[here] = (k * seen + spare * (1.0 - seen)).astype(jnp.bfloat16)
            v = (v * seen).astype(jnp.bfloat16)
            for h in range(HEADS_CHUNK):
                values[h, here, 0:HD] = v[:, h * HD : (h + 1) * HD]
            return carry

        lax.fori_loop(0, groups, block, 0)

    def attend(j, h):
        feature = lanes(h * HD, HD)
        tile = rows_all // 2
        k = keys[:, feature]
        lane = lax.broadcasted_iota(jnp.int32, (tile, 128), 1)
        for part in range(2):
            place = slice(part * tile, (part + 1) * tile)
            q = queries[j, place, feature]
            scores = lax.dot_general(q, k, (((1,), (1,)), ((), ())), preferred_element_type=jnp.float32)
            row_max = jnp.max(scores, axis=1, keepdims=True) * SCALE
            weights = jnp.exp2(scores * SCALE - row_max)
            mixed = jnp.dot(weights.astype(jnp.bfloat16), values[h], preferred_element_type=jnp.float32)
            total = mixed[:, HD:]
            partial[j, place, feature] = (mixed[:, :HD] / total).astype(jnp.bfloat16)
            stats_col[place, :] = jnp.where(lane == h, row_max + jnp.log2(total), stats_col[place, :])

    def tables(i, carry):
        video, own_video = video_ref[i], video_ref[rep]
        limit = counts_ref[own_video] * (tokens * 8)
        row, seen = jnp.int32(0), jnp.float32(0.0)
        for b in range(blocks):
            held, own = slot_ref[video, b], slot_ref[own_video, b]
            row += jnp.where(held // rows_held == rep, held % rows_held, 0)
            seen += jnp.where((own // rows_held == i) & (b * tokens < limit), 1.0, 0.0)
        sel_ref[i] = row
        vis_ref[i] = seen
        return carry

    barrier = pltpu.get_barrier_semaphore()
    peers = [(2 * x + h, group_at(k)) for k in range(len(ORDER)) for h in range(2)]
    peers += [(2 * x + other, rep)] + [(2 * to + h, rep) for to in (right, left) for h in range(2)]
    for peer in peers:
        pl.semaphore_signal(barrier, inc=1, device_id=peer, device_id_type=MESH)
    loads = [pltpu.make_async_copy(qkv_ref.at[i], qk.at[i], load_sem.at[i]) for i in range(2)]
    loads[0].start()
    start(raw_copies(0))
    loads[1].start()
    start(raw_copies(1))
    loads[0].wait()
    normalize(0)
    pl.semaphore_wait(barrier, len(peers))
    start(first_copies(0))
    start(first_copies(1))
    lax.fori_loop(0, groups, tables, 0)
    gather(0)
    start(cache_copies(0))
    gather(1)
    start(cache_copies(1))
    for h in range(HEADS_CHUNK):
        values[h, 0:quarter, HD:] = jnp.ones((quarter, HD), jnp.bfloat16)

    def shares(owner, carry):
        count = 2 * 24
        here = pl.ds(pl.multiple_of(quarter + owner * count, 16), count)
        filled = jnp.full((count, HD), vis_ref[owner], jnp.float32).astype(jnp.bfloat16)
        for h in range(HEADS_CHUNK):
            values[h, here, HD:] = filled
        return carry

    lax.fori_loop(0, groups, shares, 0)
    stats_col[...] = jnp.zeros_like(stats_col)
    weights_row[...] = jnp.zeros_like(weights_row)
    loads[1].wait()
    normalize(1)

    def spread(j, carry):
        start(own_copies(j))
        start(kv_copies(j))
        return carry

    lax.fori_loop(0, chunks, spread, 0)

    for j in range(2, SLOTS):
        gather(j)
        start(cache_copies(j))
    wait_first(0)
    start(hop_copies(0))
    start(first_copies(2))

    def step(j, carry):
        wait_hop(j)
        wait_kv(j)
        for copy in own_copies(j):
            copy.wait()
        wait_cache(j)
        prepare(j)
        attend(j, 0)

        @pl.when(j + 1 < chunks)
        def _():
            wait_first(j + 1)
            start(hop_copies(j + 1))

        @pl.when(j + 3 < chunks)
        def _():
            start(first_copies(j + 3))

        for early in range(chunks - SLOTS):

            @pl.when(j == early)
            def _():
                for copy in cache_copies(early):
                    copy.wait_send()
                gather(early + SLOTS)
                start(cache_copies(early + SLOTS))

        def rest(h, inner):
            attend(j, h)
            return inner

        lax.fori_loop(1, HEADS_CHUNK, rest, 0)
        for d in range(4):
            stats[j, d] = jnp.transpose(stats_col[d * quarter : (d + 1) * quarter, :])[0:8]
        start(s1_copies(j))

        @pl.when(j >= 1)
        def _():
            forward_partial(j - 1)

        @pl.when(j >= 2)
        def _():
            finish(j - 2)

        return carry

    lax.fori_loop(0, chunks, step, 0)
    forward_partial(chunks - 1)
    finish(chunks - 2)
    finish(chunks - 1)

    def drain(j, carry):
        @pl.when(j + SLOTS >= chunks)
        def _():
            for copy in cache_copies(j):
                copy.wait_send()

        for copy in first_copies(j) + hop_copies(j) + kv_copies(j) + s1_copies(j) + s2_copies(j, 0) + s2_copies(j, 1):
            copy.wait_send()
        sent, kept = out_copies(j)
        sent.wait_send()
        sent.wait_recv()
        kept.wait()
        return carry

    lax.fori_loop(0, chunks, drain, 0)


def body(stretch_qkv, norm_gains, cache, cached_stretches, block_slot, video_of_group):
    groups = lax.axis_size("rep")
    _, tokens, _, width = stretch_qkv.shape
    slots = cache.shape[0]
    stretch = tokens * lax.axis_size("wide")
    chunks = width // 2 // CHUNK
    bf16, f32 = jnp.bfloat16, jnp.float32
    rows_all = stretch
    quarter = 2 * tokens
    keys_count = quarter + groups * 2 * cache.shape[2]
    vmem, dma = pltpu.VMEM, pltpu.SemaphoreType.DMA
    peers = 2 * len(ORDER) + 1
    smem_spec = pl.BlockSpec(memory_space=pltpu.SMEM)
    any_spec = pl.BlockSpec(memory_space=pl.ANY)
    out = pl.pallas_call(
        kernel,
        name="attend_exchange",
        out_shape=jax.ShapeDtypeStruct((tokens, width), bf16),
        in_specs=[smem_spec, smem_spec, smem_spec, any_spec, pl.BlockSpec(memory_space=vmem), any_spec],
        out_specs=any_spec,
        scratch_shapes=[
            vmem((2, tokens, width), bf16),
            vmem((2, slots, 2, 3, 8, CHUNK), bf16),
            vmem((2, slots, 2, 3, 8, CHUNK), bf16),
            vmem((SLOTS, groups, 2, 2, 3, 8, CHUNK), bf16),
            vmem((chunks, groups, 2, 2, 3, 8, CHUNK), bf16),
            vmem((chunks, rows_all, CHUNK), bf16),
            vmem((chunks, quarter, CHUNK), bf16),
            vmem((chunks, quarter, CHUNK), bf16),
            vmem((keys_count, CHUNK), bf16),
            vmem((HEADS_CHUNK, keys_count, 2 * HD), bf16),
            vmem((chunks, rows_all, CHUNK), bf16),
            vmem((chunks, 2, tokens, CHUNK), bf16),
            vmem((chunks, 2, quarter, CHUNK), bf16),
            vmem((rows_all, 128), f32),
            vmem((chunks, 4, 8, quarter), f32),
            vmem((chunks, 2, 8, quarter), f32),
            vmem((chunks, 2, 8, quarter), f32),
            vmem((128, quarter), f32),
            pltpu.SMEM((groups,), jnp.int32),
            pltpu.SMEM((groups,), f32),
            dma((2,)),
            dma((2, 2)),
            dma((chunks, 3)),
            dma((chunks, peers)),
            dma((chunks, 2 * groups)),
            dma((chunks, 5)),
            dma((chunks, 5)),
            dma((chunks, 2)),
            dma((chunks, 2)),
            dma((chunks, 2)),
            dma((chunks, 2)),
            dma((chunks, 4)),
            dma((chunks, 4)),
            dma((chunks, 4)),
            dma((chunks, 4)),
            dma((chunks,)),
            dma((chunks,)),
            dma((chunks,)),
        ],
        compiler_params=pltpu.CompilerParams(collective_id=0, has_side_effects=True, vmem_limit_bytes=67043328),
    )(cached_stretches, block_slot, video_of_group, jnp.transpose(stretch_qkv[0], (1, 0, 2)), norm_gains, cache.reshape(slots, 2, 3, 8, width))
    return out[None]


def solution(mesh):
    in_specs = (P("rep", "wide", None, None), P(), P("rep", None, "wide", None), P(), P(), P())
    out_specs = P("rep", "wide", None)
    return jax.shard_map(body, mesh=mesh, in_specs=in_specs, out_specs=out_specs, check_vma=False)
```

```python
import functools
import math

import jax
import jax.numpy as jnp
from jax import lax
from jax.experimental import pallas as pl
from jax.experimental.pallas import tpu as pltpu
from jax.sharding import PartitionSpec as P

MESH = pl.DeviceIdType.MESH
HD = 128
HEADS_CHUNK = 4
SLOTS = 3
CHUNK = HD * HEADS_CHUNK
EPSILON = 1e-06
SCALE = math.log2(math.e) / math.sqrt(HD)
ORDER = ((1, 0), (0, 1), (3, 2), (2, 3), (3, 0), (0, 3), (1, 2), (2, 1), (2, 0), (0, 2), (1, 1), (3, 3), (1, 3), (3, 1), (2, 2))


def lanes(start, size):
    return pl.ds(pl.multiple_of(start, 128), size)


def kernel(
    counts_ref, slot_ref, video_ref, qkv_ref, gains_ref, cache_ref, out_ref,
    qk, raw_even, raw_odd, gathered, arrived, queries, keys_new, values_new, keys, values, partial, relay_in, final_in,
    stats_col, stats, relay_stats, final_stats, weights_row, sel_ref, vis_ref,
    load_sem, raw_sem, own_sem, cache_send, cache_recv, first_send, first_recv, hop_send, hop_recv,
    kv_send, kv_recv, s1_send, s1_recv, s2_send, s2_recv, out_send, out_recv, out_own, rows_sem,
):
    wide, rep = lax.axis_index("wide"), lax.axis_index("rep")
    x, core = wide // 2, wide % 2
    y, z = rep // 4, rep % 4
    other = 1 - core
    right, left = (x + 1) % 4, (x + 3) % 4
    chunks, rows_all, _ = queries.shape
    tokens = qk.shape[1]
    quarter = 2 * tokens
    half_width = chunks * CHUNK
    groups, blocks = slot_ref.shape
    rows_held = cache_ref.shape[0]
    raws = (raw_even, raw_odd)

    def remote(src, dst, send, recv, to_wide, to_rep):
        return pltpu.make_async_remote_copy(
            src_ref=src, dst_ref=dst, send_sem=send, recv_sem=recv, device_id=(to_wide, to_rep), device_id_type=MESH
        )

    def group_at(k):
        dy, dz = ORDER[k]
        sign = 1 - 2 * core
        return ((y + dy * sign + 4) % 4) * 4 + (z + dz * sign + 4) % 4

    def cache_copies(j):
        copies = []
        for k in range(len(ORDER)):
            to = group_at(k)
            for h in range(2):
                copies.append(remote(
                    gathered.at[j % SLOTS, to, h], arrived.at[j, rep, core], cache_send.at[j, 2 * k + h],
                    cache_recv.at[j, rep * 2 + core], 2 * x + h, to))
        copies.append(remote(
            gathered.at[j % SLOTS, rep, other], arrived.at[j, rep, core], cache_send.at[j, 2 * len(ORDER)],
            cache_recv.at[j, rep * 2 + core], 2 * x + other, rep))
        return copies

    def wait_cache(j):
        for k in range(len(ORDER)):
            owner = group_at(k)
            for h in range(2):
                remote(gathered.at[0, 0, 0], arrived.at[j, owner, h], cache_send.at[j, 0],
                       cache_recv.at[j, owner * 2 + h], wide, rep).wait_recv()
        remote(gathered.at[0, 0, 0], arrived.at[j, rep, other], cache_send.at[j, 0],
               cache_recv.at[j, rep * 2 + other], wide, rep).wait_recv()

    def piece(j, position):
        return queries.at[j, pl.ds(pl.multiple_of(position * tokens, 16), tokens)]

    def own_columns(h, j):
        return lanes(h * half_width + j * CHUNK, CHUNK)

    def first_copies(j):
        copies = [remote(qk.at[0, :, own_columns(other, j)], piece(j, wide), first_send.at[j, 0], first_recv.at[j, 0],
                         2 * x + other, rep)]
        for side, to in enumerate((right, left)):
            for h in range(2):
                copies.append(remote(
                    qk.at[0, :, own_columns(h, j)], piece(j, wide), first_send.at[j, 1 + 2 * side + h],
                    first_recv.at[j, 1 + 2 * side + core], 2 * to + h, rep))
        return copies

    def wait_first(j):
        sources = [2 * x + other, 2 * left, 2 * left + 1, 2 * right, 2 * right + 1]
        for slot, source in enumerate(sources):
            remote(piece(j, wide), piece(j, source), first_send.at[j, 0], first_recv.at[j, slot], wide, rep).wait_recv()

    def hop_copies(j):
        return [
            remote(piece(j, 2 * left), piece(j, 2 * left), hop_send.at[j, 0], hop_recv.at[j, 0], 2 * right + core, rep),
            remote(piece(j, 2 * right + 1), piece(j, 2 * right + 1), hop_send.at[j, 1], hop_recv.at[j, 1], 2 * left + core, rep),
        ]

    def wait_hop(j):
        far = (x + 2) % 4
        for slot in range(2):
            remote(piece(j, wide), piece(j, 2 * far + slot), hop_send.at[j, 0], hop_recv.at[j, slot], wide, rep).wait_recv()

    def token_rows(c):
        return pl.ds(pl.multiple_of(c * tokens, 16), tokens)

    def kv_copies(j):
        return [
            remote(qk.at[1, :, own_columns(other, j)], keys_new.at[j, token_rows(core)], kv_send.at[j, 0], kv_recv.at[j, 0],
                   2 * x + other, rep),
            remote(qkv_ref.at[2, :, own_columns(other, j)], values_new.at[j, token_rows(core)], kv_send.at[j, 1],
                   kv_recv.at[j, 1], 2 * x + other, rep),
        ]

    def wait_kv(j):
        remote(keys_new.at[j, token_rows(core)], keys_new.at[j, token_rows(other)], kv_send.at[j, 0], kv_recv.at[j, 0],
               wide, rep).wait_recv()
        remote(keys_new.at[j, token_rows(core)], values_new.at[j, token_rows(other)], kv_send.at[j, 1], kv_recv.at[j, 1],
               wide, rep).wait_recv()

    def own_copies(j):
        return [
            pltpu.make_async_copy(qk.at[0, :, own_columns(core, j)], piece(j, wide), own_sem.at[j, 0]),
            pltpu.make_async_copy(qk.at[1, :, own_columns(core, j)], keys_new.at[j, token_rows(core)], own_sem.at[j, 1]),
            pltpu.make_async_copy(qkv_ref.at[2, :, own_columns(core, j)], values_new.at[j, token_rows(core)], own_sem.at[j, 2]),
        ]

    def raw_copies(j):
        return [
            pltpu.make_async_copy(cache_ref.at[:, :, :, :, own_columns(h, j)], raws[j % 2].at[h], raw_sem.at[j % 2, h])
            for h in range(2)
        ]

    def gather(j):
        for copy in raw_copies(j):
            copy.wait()

        def place(to, carry):
            row = sel_ref[to]
            for h in range(2):
                gathered[j % SLOTS, to, h] = raws[j % 2][h, row]
            return carry

        lax.fori_loop(0, groups, place, 0)
        arrived[j, rep, core] = raws[j % 2][core, sel_ref[rep]]

        if j + 2 < chunks:
            start(raw_copies(j + 2))

    def normalize(which):
        def rows_step(i, carry):
            block = pl.ds(pl.multiple_of(i * 16, 16), 16)
            widened = qk[which, block, :].astype(jnp.float32)
            mean_square = jnp.mean(widened * widened, axis=-1, keepdims=True)
            scaled = widened * lax.rsqrt(mean_square + EPSILON) * gains_ref[which : which + 1, :]
            qk[which, block, :] = scaled.astype(jnp.bfloat16)
            return carry

        lax.fori_loop(0, tokens // 16, rows_step, 0)

    def start(copies):
        for copy in copies:
            copy.start()

    def quarter_rows(d):
        return pl.ds(pl.multiple_of(d * quarter, 16), quarter)

    def half_rows(d, part):
        return pl.ds(pl.multiple_of(d * quarter + part * tokens, 16), tokens)

    def s1_copies(j):
        far = (x + 2) % 4
        copies = []
        for slot, to in enumerate((right, left)):
            copies.append(remote(partial.at[j, half_rows(far, 1 - slot)], relay_in.at[j, slot], s1_send.at[j, 2 * slot],
                                 s1_recv.at[j, 2 * slot], 2 * to + core, rep))
            copies.append(remote(stats.at[j, far], relay_stats.at[j, slot], s1_send.at[j, 2 * slot + 1],
                                 s1_recv.at[j, 2 * slot + 1], 2 * to + core, rep))
        return copies

    def s2_copies(j, slot):
        to = (right, left)[slot]
        return [
            remote(partial.at[j, quarter_rows(to)], final_in.at[j, slot], s2_send.at[j, 2 * slot], s2_recv.at[j, 2 * slot],
                   2 * to + core, rep),
            remote(stats.at[j, to], final_stats.at[j, slot], s2_send.at[j, 2 * slot + 1], s2_recv.at[j, 2 * slot + 1],
                   2 * to + core, rep),
        ]

    def forward_partial(j):
        for slot, to in enumerate((right, left)):
            remote(relay_in.at[j, slot], relay_in.at[j, slot], s1_send.at[j, 0], s1_recv.at[j, 2 * slot], wide, rep).wait_recv()
            remote(relay_stats.at[j, slot], relay_stats.at[j, slot], s1_send.at[j, 0], s1_recv.at[j, 2 * slot + 1], wide,
                   rep).wait_recv()
            here, came = stats[j, to], relay_stats[j, slot]
            top = jnp.maximum(here, came)
            a, b = jnp.exp2(here - top), jnp.exp2(came - top)
            total = a + b
            token = lax.broadcasted_iota(jnp.int32, here.shape, 1)
            merged = token >= tokens if slot == 0 else token < tokens
            stats[j, to] = jnp.where(merged, top + jnp.log2(total), here)
            weights_row[0:8] = a / total
            weights_row[8:16] = b / total
            part = 1 - slot
            columns = jnp.transpose(weights_row[...])[part * tokens : (part + 1) * tokens]
            place = half_rows(to, part)
            for h in range(HEADS_CHUNK):
                feature = slice(h * HD, (h + 1) * HD)
                mixed = columns[:, h : h + 1] * partial[j, place, feature].astype(jnp.float32)
                mixed += columns[:, 8 + h : 9 + h] * relay_in[j, slot, :, feature].astype(jnp.float32)
                partial[j, place, feature] = mixed.astype(jnp.bfloat16)
            start(s2_copies(j, slot))

    def out_copies(j):
        place = own_columns(core, j)
        return (
            remote(partial.at[j, half_rows(x, other)], out_ref.at[:, place], out_send.at[j], out_recv.at[j], 2 * x + other, rep),
            pltpu.make_async_copy(partial.at[j, half_rows(x, core)], out_ref.at[:, place], out_own.at[j]),
        )

    def finish(j):
        for slot in range(2):
            remote(final_in.at[j, slot], final_in.at[j, slot], s2_send.at[j, 0], s2_recv.at[j, 2 * slot], wide, rep).wait_recv()
            remote(final_stats.at[j, slot], final_stats.at[j, slot], s2_send.at[j, 0], s2_recv.at[j, 2 * slot + 1], wide,
                   rep).wait_recv()
        here, first, second = stats[j, x], final_stats[j, 0], final_stats[j, 1]
        top = jnp.maximum(here, jnp.maximum(first, second))
        a, b, c = jnp.exp2(here - top), jnp.exp2(first - top), jnp.exp2(second - top)
        total = a + b + c
        weights_row[0:8] = a / total
        weights_row[8:16] = b / total
        weights_row[16:24] = c / total
        columns = jnp.transpose(weights_row[...])
        place = quarter_rows(x)
        for h in range(HEADS_CHUNK):
            feature = slice(h * HD, (h + 1) * HD)
            mixed = columns[:, h : h + 1] * partial[j, place, feature].astype(jnp.float32)
            mixed += columns[:, 8 + h : 9 + h] * final_in[j, 0, :, feature].astype(jnp.float32)
            mixed += columns[:, 16 + h : 17 + h] * final_in[j, 1, :, feature].astype(jnp.float32)
            partial[j, place, feature] = mixed.astype(jnp.bfloat16)
        start(out_copies(j))

    def prepare(j):
        keys[0:quarter] = keys_new[j]
        for h in range(HEADS_CHUNK):
            values[h, 0:quarter, 0:HD] = values_new[j, :, h * HD : (h + 1) * HD]
        rows = quarter // 8

        def block(owner, carry):
            seen = vis_ref[owner]
            count = 2 * 24
            here = pl.ds(pl.multiple_of(quarter + owner * count, 16), count)
            spare = keys_new[j, 0:count].astype(jnp.float32)
            k = arrived[j, owner, :, 0].astype(jnp.float32).reshape(count, CHUNK)
            v = arrived[j, owner, :, 1].astype(jnp.float32).reshape(count, CHUNK)
            keys[here] = (k * seen + spare * (1.0 - seen)).astype(jnp.bfloat16)
            v = (v * seen).astype(jnp.bfloat16)
            for h in range(HEADS_CHUNK):
                values[h, here, 0:HD] = v[:, h * HD : (h + 1) * HD]
            return carry

        lax.fori_loop(0, groups, block, 0)

    def attend(j, h):
        feature = lanes(h * HD, HD)
        tile = rows_all // 2
        k = keys[:, feature]
        lane = lax.broadcasted_iota(jnp.int32, (tile, 128), 1)
        for part in range(2):
            place = slice(part * tile, (part + 1) * tile)
            q = queries[j, place, feature]
            scores = lax.dot_general(q, k, (((1,), (1,)), ((), ())), preferred_element_type=jnp.float32)
            row_max = jnp.max(scores, axis=1, keepdims=True) * SCALE
            weights = jnp.exp2(scores * SCALE - row_max)
            mixed = jnp.dot(weights.astype(jnp.bfloat16), values[h], preferred_element_type=jnp.float32)
            total = mixed[:, HD:]
            partial[j, place, feature] = (mixed[:, :HD] / total).astype(jnp.bfloat16)
            stats_col[place, :] = jnp.where(lane == h, row_max + jnp.log2(total), stats_col[place, :])

    def tables(i, carry):
        video, own_video = video_ref[i], video_ref[rep]
        limit = counts_ref[own_video] * (tokens * 8)
        row, seen = jnp.int32(0), jnp.float32(0.0)
        for b in range(blocks):
            held, own = slot_ref[video, b], slot_ref[own_video, b]
            row += jnp.where(held // rows_held == rep, held % rows_held, 0)
            seen += jnp.where((own // rows_held == i) & (b * tokens < limit), 1.0, 0.0)
        sel_ref[i] = row
        vis_ref[i] = seen
        return carry

    barrier = pltpu.get_barrier_semaphore()
    column = [(wide, ((y + d) % 4) * 4 + z) for d in range(1, 4)]
    peers = [(2 * x + h, y * 4 + (z + d) % 4) for d in range(1, 4) for h in range(2)] + column
    peers += [(2 * x + other, rep)] + [(2 * to + h, rep) for to in (right, left) for h in range(2)]
    for peer in peers:
        pl.semaphore_signal(barrier, inc=1, device_id=peer, device_id_type=MESH)
    loads = [pltpu.make_async_copy(qkv_ref.at[i], qk.at[i], load_sem.at[i]) for i in range(2)]
    loads[0].start()
    start(raw_copies(0))
    loads[1].start()
    start(raw_copies(1))
    lax.fori_loop(0, groups, tables, 0)
    loads[0].wait()
    normalize(0)
    pl.semaphore_wait(barrier, len(peers))
    for peer in column:
        pl.semaphore_signal(rows_sem, inc=1, device_id=peer, device_id_type=MESH)
    start(first_copies(0))
    start(first_copies(1))
    gather(0)
    pl.semaphore_wait(rows_sem, len(column))
    start(cache_copies(0))
    gather(1)
    start(cache_copies(1))
    for h in range(HEADS_CHUNK):
        values[h, 0:quarter, HD:] = jnp.ones((quarter, HD), jnp.bfloat16)

    def shares(owner, carry):
        count = 2 * 24
        here = pl.ds(pl.multiple_of(quarter + owner * count, 16), count)
        filled = jnp.full((count, HD), vis_ref[owner], jnp.float32).astype(jnp.bfloat16)
        for h in range(HEADS_CHUNK):
            values[h, here, HD:] = filled
        return carry

    lax.fori_loop(0, groups, shares, 0)
    stats_col[...] = jnp.zeros_like(stats_col)
    weights_row[...] = jnp.zeros_like(weights_row)
    loads[1].wait()
    normalize(1)

    def spread(j, carry):
        start(own_copies(j))
        start(kv_copies(j))
        return carry

    lax.fori_loop(0, chunks, spread, 0)

    for j in range(2, SLOTS):
        gather(j)
        start(cache_copies(j))
    wait_first(0)
    start(hop_copies(0))
    start(first_copies(2))

    def step(j, carry):
        wait_hop(j)
        wait_kv(j)
        for copy in own_copies(j):
            copy.wait()
        wait_cache(j)
        prepare(j)
        attend(j, 0)

        @pl.when(j + 1 < chunks)
        def _():
            wait_first(j + 1)
            start(hop_copies(j + 1))

        @pl.when(j + 3 < chunks)
        def _():
            start(first_copies(j + 3))

        for early in range(chunks - SLOTS):

            @pl.when(j == early)
            def _():
                for copy in cache_copies(early):
                    copy.wait_send()
                gather(early + SLOTS)
                start(cache_copies(early + SLOTS))

        def rest(h, inner):
            attend(j, h)
            return inner

        lax.fori_loop(1, HEADS_CHUNK, rest, 0)
        for d in range(4):
            stats[j, d] = jnp.transpose(stats_col[d * quarter : (d + 1) * quarter, :])[0:8]
        start(s1_copies(j))

        @pl.when(j >= 1)
        def _():
            forward_partial(j - 1)

        @pl.when(j >= 2)
        def _():
            finish(j - 2)

        return carry

    lax.fori_loop(0, chunks, step, 0)
    forward_partial(chunks - 1)
    finish(chunks - 2)
    finish(chunks - 1)

    def drain(j, carry):
        @pl.when(j + SLOTS >= chunks)
        def _():
            for copy in cache_copies(j):
                copy.wait_send()

        for copy in first_copies(j) + hop_copies(j) + kv_copies(j) + s1_copies(j) + s2_copies(j, 0) + s2_copies(j, 1):
            copy.wait_send()
        sent, kept = out_copies(j)
        sent.wait_send()
        sent.wait_recv()
        kept.wait()
        return carry

    lax.fori_loop(0, chunks, drain, 0)


def deliver_kernel(src_ref, dst_ref, held, in_sem, out_sem):
    parts = held.shape[0]
    rows = held.shape[1]
    loads = [pltpu.make_async_copy(src_ref.at[i * rows : (i + 1) * rows], held.at[i], in_sem.at[i]) for i in range(parts)]
    stores = [pltpu.make_async_copy(held.at[i], dst_ref.at[i * rows : (i + 1) * rows], out_sem.at[i]) for i in range(parts)]
    for load in loads:
        load.start()
    for load, store in zip(loads, stores):
        load.wait()
        store.start()
    for store in stores:
        store.wait()


def deliver(array):
    parts = 6
    rows, width = array.shape
    any_spec = pl.BlockSpec(memory_space=pl.ANY)
    return pl.pallas_call(
        deliver_kernel,
        name="deliver",
        out_shape=jax.ShapeDtypeStruct(array.shape, array.dtype),
        in_specs=[any_spec],
        out_specs=any_spec,
        scratch_shapes=[
            pltpu.VMEM((parts, rows // parts, width), array.dtype),
            pltpu.SemaphoreType.DMA((parts,)),
            pltpu.SemaphoreType.DMA((parts,)),
        ],
        compiler_params=pltpu.CompilerParams(vmem_limit_bytes=60 << 20),
    )(array)


def body(stretch_qkv, norm_gains, cache, cached_stretches, block_slot, video_of_group):
    groups = lax.axis_size("rep")
    _, tokens, _, width = stretch_qkv.shape
    slots = cache.shape[0]
    stretch = tokens * lax.axis_size("wide")
    chunks = width // 2 // CHUNK
    bf16, f32 = jnp.bfloat16, jnp.float32
    rows_all = stretch
    quarter = 2 * tokens
    keys_count = quarter + groups * 2 * cache.shape[2]
    vmem, dma = pltpu.VMEM, pltpu.SemaphoreType.DMA
    peers = 2 * len(ORDER) + 1
    smem_spec = pl.BlockSpec(memory_space=pltpu.SMEM)
    any_spec = pl.BlockSpec(memory_space=pl.ANY)
    out = pl.pallas_call(
        kernel,
        name="attend_exchange",
        out_shape=jax.ShapeDtypeStruct((tokens, width), bf16),
        in_specs=[smem_spec, smem_spec, smem_spec, any_spec, pl.BlockSpec(memory_space=vmem), any_spec],
        out_specs=any_spec,
        scratch_shapes=[
            vmem((2, tokens, width), bf16),
            vmem((2, slots, 2, 3, 8, CHUNK), bf16),
            vmem((2, slots, 2, 3, 8, CHUNK), bf16),
            vmem((SLOTS, groups, 2, 2, 3, 8, CHUNK), bf16),
            vmem((chunks, groups, 2, 2, 3, 8, CHUNK), bf16),
            vmem((chunks, rows_all, CHUNK), bf16),
            vmem((chunks, quarter, CHUNK), bf16),
            vmem((chunks, quarter, CHUNK), bf16),
            vmem((keys_count, CHUNK), bf16),
            vmem((HEADS_CHUNK, keys_count, 2 * HD), bf16),
            vmem((chunks, rows_all, CHUNK), bf16),
            vmem((chunks, 2, tokens, CHUNK), bf16),
            vmem((chunks, 2, quarter, CHUNK), bf16),
            vmem((rows_all, 128), f32),
            vmem((chunks, 4, 8, quarter), f32),
            vmem((chunks, 2, 8, quarter), f32),
            vmem((chunks, 2, 8, quarter), f32),
            vmem((128, quarter), f32),
            pltpu.SMEM((groups,), jnp.int32),
            pltpu.SMEM((groups,), f32),
            dma((2,)),
            dma((2, 2)),
            dma((chunks, 3)),
            dma((chunks, peers)),
            dma((chunks, 2 * groups)),
            dma((chunks, 5)),
            dma((chunks, 5)),
            dma((chunks, 2)),
            dma((chunks, 2)),
            dma((chunks, 2)),
            dma((chunks, 2)),
            dma((chunks, 4)),
            dma((chunks, 4)),
            dma((chunks, 4)),
            dma((chunks, 4)),
            dma((chunks,)),
            dma((chunks,)),
            dma((chunks,)),
            pltpu.SemaphoreType.REGULAR,
        ],
        compiler_params=pltpu.CompilerParams(collective_id=0, has_side_effects=True, vmem_limit_bytes=67043328),
    )(cached_stretches, block_slot, video_of_group, jnp.transpose(stretch_qkv[0], (1, 0, 2)), norm_gains, cache.reshape(slots, 2, 3, 8, width))
    return deliver(out)[None]


def solution(mesh):
    in_specs = (P("rep", "wide", None, None), P(), P("rep", None, "wide", None), P(), P(), P())
    out_specs = P("rep", "wide", None)
    return jax.shard_map(body, mesh=mesh, in_specs=in_specs, out_specs=out_specs, check_vma=False)
```

```python
import functools
import math

import jax
import jax.numpy as jnp
from jax import lax
from jax.experimental import pallas as pl
from jax.experimental.pallas import tpu as pltpu
from jax.sharding import PartitionSpec as P

MESH = pl.DeviceIdType.MESH
HD = 128
HEADS_CHUNK = 4
SLOTS = 3
CHUNK = HD * HEADS_CHUNK
EPSILON = 1e-06
SCALE = math.log2(math.e) / math.sqrt(HD)
ORDER = ((1, 0), (0, 1), (3, 2), (2, 3), (3, 0), (0, 3), (1, 2), (2, 1), (2, 0), (0, 2), (1, 1), (3, 3), (1, 3), (3, 1), (2, 2))


def lanes(start, size):
    return pl.ds(pl.multiple_of(start, 128), size)


def kernel(
    counts_ref, slot_ref, video_ref, qkv_ref, gains_ref, cache_ref, out_ref,
    qk, raw_even, raw_odd, gathered, arrived, queries, keys_new, values_new, keys, values, partial, relay_in, final_in,
    stats_col, stats, relay_stats, final_stats, weights_row, columns_row, sel_ref, vis_ref,
    load_sem, raw_sem, own_sem, cache_send, cache_recv, first_send, first_recv, hop_send, hop_recv,
    kv_send, kv_recv, s1_send, s1_recv, s2_send, s2_recv, out_send, out_recv, out_own, rows_sem,
):
    wide, rep = lax.axis_index("wide"), lax.axis_index("rep")
    x, core = wide // 2, wide % 2
    y, z = rep // 4, rep % 4
    other = 1 - core
    right, left = (x + 1) % 4, (x + 3) % 4
    chunks, rows_all, _ = queries.shape
    tokens = qk.shape[1]
    quarter = 2 * tokens
    half_width = chunks * CHUNK
    groups, blocks = slot_ref.shape
    rows_held = cache_ref.shape[0]
    raws = (raw_even, raw_odd)

    def remote(src, dst, send, recv, to_wide, to_rep):
        return pltpu.make_async_remote_copy(
            src_ref=src, dst_ref=dst, send_sem=send, recv_sem=recv, device_id=(to_wide, to_rep), device_id_type=MESH
        )

    def group_at(k):
        dy, dz = ORDER[k]
        sign = 1 - 2 * core
        return ((y + dy * sign + 4) % 4) * 4 + (z + dz * sign + 4) % 4

    def cache_copies(j):
        copies = []
        for k in range(len(ORDER)):
            to = group_at(k)
            for h in range(2):
                copies.append(remote(
                    gathered.at[j % SLOTS, to, h], arrived.at[j, rep, core], cache_send.at[j, 2 * k + h],
                    cache_recv.at[j, rep * 2 + core], 2 * x + h, to))
        copies.append(remote(
            gathered.at[j % SLOTS, rep, other], arrived.at[j, rep, core], cache_send.at[j, 2 * len(ORDER)],
            cache_recv.at[j, rep * 2 + core], 2 * x + other, rep))
        return copies

    def wait_cache(j):
        for k in range(len(ORDER)):
            owner = group_at(k)
            for h in range(2):
                remote(gathered.at[0, 0, 0], arrived.at[j, owner, h], cache_send.at[j, 0],
                       cache_recv.at[j, owner * 2 + h], wide, rep).wait_recv()
        remote(gathered.at[0, 0, 0], arrived.at[j, rep, other], cache_send.at[j, 0],
               cache_recv.at[j, rep * 2 + other], wide, rep).wait_recv()

    def piece(j, position):
        return queries.at[j, pl.ds(pl.multiple_of(position * tokens, 16), tokens)]

    def own_columns(h, j):
        return lanes(h * half_width + j * CHUNK, CHUNK)

    def first_copies(j):
        copies = [remote(qk.at[0, :, own_columns(other, j)], piece(j, wide), first_send.at[j, 0], first_recv.at[j, 0],
                         2 * x + other, rep)]
        for side, to in enumerate((right, left)):
            for h in range(2):
                copies.append(remote(
                    qk.at[0, :, own_columns(h, j)], piece(j, wide), first_send.at[j, 1 + 2 * side + h],
                    first_recv.at[j, 1 + 2 * side + core], 2 * to + h, rep))
        return copies

    def wait_first(j):
        sources = [2 * x + other, 2 * left, 2 * left + 1, 2 * right, 2 * right + 1]
        for slot, source in enumerate(sources):
            remote(piece(j, wide), piece(j, source), first_send.at[j, 0], first_recv.at[j, slot], wide, rep).wait_recv()

    def hop_copies(j):
        return [
            remote(piece(j, 2 * left), piece(j, 2 * left), hop_send.at[j, 0], hop_recv.at[j, 0], 2 * right + core, rep),
            remote(piece(j, 2 * right + 1), piece(j, 2 * right + 1), hop_send.at[j, 1], hop_recv.at[j, 1], 2 * left + core, rep),
        ]

    def wait_hop(j):
        far = (x + 2) % 4
        for slot in range(2):
            remote(piece(j, wide), piece(j, 2 * far + slot), hop_send.at[j, 0], hop_recv.at[j, slot], wide, rep).wait_recv()

    def token_rows(c):
        return pl.ds(pl.multiple_of(c * tokens, 16), tokens)

    def kv_copies(j):
        return [
            remote(qk.at[1, :, own_columns(other, j)], keys_new.at[j, token_rows(core)], kv_send.at[j, 0], kv_recv.at[j, 0],
                   2 * x + other, rep),
            remote(qkv_ref.at[2, :, own_columns(other, j)], values_new.at[j, token_rows(core)], kv_send.at[j, 1],
                   kv_recv.at[j, 1], 2 * x + other, rep),
        ]

    def wait_kv(j):
        remote(keys_new.at[j, token_rows(core)], keys_new.at[j, token_rows(other)], kv_send.at[j, 0], kv_recv.at[j, 0],
               wide, rep).wait_recv()
        remote(keys_new.at[j, token_rows(core)], values_new.at[j, token_rows(other)], kv_send.at[j, 1], kv_recv.at[j, 1],
               wide, rep).wait_recv()

    def own_copies(j):
        return [
            pltpu.make_async_copy(qk.at[0, :, own_columns(core, j)], piece(j, wide), own_sem.at[j, 0]),
            pltpu.make_async_copy(qk.at[1, :, own_columns(core, j)], keys_new.at[j, token_rows(core)], own_sem.at[j, 1]),
            pltpu.make_async_copy(qkv_ref.at[2, :, own_columns(core, j)], values_new.at[j, token_rows(core)], own_sem.at[j, 2]),
        ]

    def raw_copies(j):
        return [
            pltpu.make_async_copy(cache_ref.at[:, :, :, :, own_columns(h, j)], raws[j % 2].at[h], raw_sem.at[j % 2, h])
            for h in range(2)
        ]

    def gather(j):
        for copy in raw_copies(j):
            copy.wait()

        def place(to, carry):
            row = sel_ref[to]
            for h in range(2):
                gathered[j % SLOTS, to, h] = raws[j % 2][h, row]
            return carry

        lax.fori_loop(0, groups, place, 0)
        arrived[j, rep, core] = raws[j % 2][core, sel_ref[rep]]

        if j + 2 < chunks:
            start(raw_copies(j + 2))

    def normalize(which):
        def rows_step(i, carry):
            block = pl.ds(pl.multiple_of(i * 16, 16), 16)
            widened = qk[which, block, :].astype(jnp.float32)
            mean_square = jnp.mean(widened * widened, axis=-1, keepdims=True)
            scaled = widened * lax.rsqrt(mean_square + EPSILON) * gains_ref[which : which + 1, :]
            qk[which, block, :] = scaled.astype(jnp.bfloat16)
            return carry

        lax.fori_loop(0, tokens // 16, rows_step, 0)

    def start(copies):
        for copy in copies:
            copy.start()

    def quarter_rows(d):
        return pl.ds(pl.multiple_of(d * quarter, 16), quarter)

    def half_rows(d, part):
        return pl.ds(pl.multiple_of(d * quarter + part * tokens, 16), tokens)

    def s1_copies(j):
        far = (x + 2) % 4
        copies = []
        for slot, to in enumerate((right, left)):
            copies.append(remote(partial.at[j, half_rows(far, 1 - slot)], relay_in.at[j, slot], s1_send.at[j, 2 * slot],
                                 s1_recv.at[j, 2 * slot], 2 * to + core, rep))
            copies.append(remote(stats.at[j, far], relay_stats.at[j, slot], s1_send.at[j, 2 * slot + 1],
                                 s1_recv.at[j, 2 * slot + 1], 2 * to + core, rep))
        return copies

    def s2_copies(j, slot):
        to = (right, left)[slot]
        return [
            remote(partial.at[j, quarter_rows(to)], final_in.at[j, slot], s2_send.at[j, 2 * slot], s2_recv.at[j, 2 * slot],
                   2 * to + core, rep),
            remote(stats.at[j, to], final_stats.at[j, slot], s2_send.at[j, 2 * slot + 1], s2_recv.at[j, 2 * slot + 1],
                   2 * to + core, rep),
        ]

    def forward_partial(j):
        for slot, to in enumerate((right, left)):
            remote(relay_in.at[j, slot], relay_in.at[j, slot], s1_send.at[j, 0], s1_recv.at[j, 2 * slot], wide, rep).wait_recv()
            remote(relay_stats.at[j, slot], relay_stats.at[j, slot], s1_send.at[j, 0], s1_recv.at[j, 2 * slot + 1], wide,
                   rep).wait_recv()
            here, came = stats[j, to], relay_stats[j, slot]
            top = jnp.maximum(here, came)
            a, b = jnp.exp2(here - top), jnp.exp2(came - top)
            total = a + b
            token = lax.broadcasted_iota(jnp.int32, here.shape, 1)
            merged = token >= tokens if slot == 0 else token < tokens
            stats[j, to] = jnp.where(merged, top + jnp.log2(total), here)
            weights_row[0:HEADS_CHUNK] = a / total
            weights_row[8 : 8 + HEADS_CHUNK] = b / total
            part = 1 - slot
            columns = jnp.transpose(weights_row[...])[part * tokens : (part + 1) * tokens]
            place = half_rows(to, part)
            for h in range(HEADS_CHUNK):
                feature = slice(h * HD, (h + 1) * HD)
                mixed = columns[:, h : h + 1] * partial[j, place, feature].astype(jnp.float32)
                mixed += columns[:, 8 + h : 9 + h] * relay_in[j, slot, :, feature].astype(jnp.float32)
                partial[j, place, feature] = mixed.astype(jnp.bfloat16)
            start(s2_copies(j, slot))

    def out_copies(j):
        place = own_columns(core, j)
        return (
            remote(partial.at[j, half_rows(x, other)], out_ref.at[:, place], out_send.at[j], out_recv.at[j], 2 * x + other, rep),
            pltpu.make_async_copy(partial.at[j, half_rows(x, core)], out_ref.at[:, place], out_own.at[j]),
        )

    def finish(j):
        for slot in range(2):
            remote(final_in.at[j, slot], final_in.at[j, slot], s2_send.at[j, 0], s2_recv.at[j, 2 * slot], wide, rep).wait_recv()
            remote(final_stats.at[j, slot], final_stats.at[j, slot], s2_send.at[j, 0], s2_recv.at[j, 2 * slot + 1], wide,
                   rep).wait_recv()
        here, first, second = stats[j, x], final_stats[j, 0], final_stats[j, 1]
        top = jnp.maximum(here, jnp.maximum(first, second))
        a, b, c = jnp.exp2(here - top), jnp.exp2(first - top), jnp.exp2(second - top)
        total = a + b + c
        weights_row[0:HEADS_CHUNK] = a / total
        weights_row[8 : 8 + HEADS_CHUNK] = b / total
        weights_row[16 : 16 + HEADS_CHUNK] = c / total
        columns_row[...] = jnp.transpose(weights_row[...])
        copies = out_copies(j)
        for copy, part in zip(copies, (other, core)):
            place, within = half_rows(x, part), token_rows(part)
            columns = columns_row[within]
            for h in range(HEADS_CHUNK):
                feature = slice(h * HD, (h + 1) * HD)
                mixed = columns[:, h : h + 1] * partial[j, place, feature].astype(jnp.float32)
                mixed += columns[:, 8 + h : 9 + h] * final_in[j, 0, within, feature].astype(jnp.float32)
                mixed += columns[:, 16 + h : 17 + h] * final_in[j, 1, within, feature].astype(jnp.float32)
                partial[j, place, feature] = mixed.astype(jnp.bfloat16)
            copy.start()

    def prepare(j):
        keys[0:quarter] = keys_new[j]
        for h in range(HEADS_CHUNK):
            values[h, 0:quarter, 0:HD] = values_new[j, :, h * HD : (h + 1) * HD]
        rows = quarter // 8

        def block(owner, carry):
            seen = vis_ref[owner]
            count = 2 * 24
            here = pl.ds(pl.multiple_of(quarter + owner * count, 16), count)
            spare = keys_new[j, 0:count].astype(jnp.float32)
            k = arrived[j, owner, :, 0].astype(jnp.float32).reshape(count, CHUNK)
            v = arrived[j, owner, :, 1].astype(jnp.float32).reshape(count, CHUNK)
            keys[here] = (k * seen + spare * (1.0 - seen)).astype(jnp.bfloat16)
            v = (v * seen).astype(jnp.bfloat16)
            for h in range(HEADS_CHUNK):
                values[h, here, 0:HD] = v[:, h * HD : (h + 1) * HD]
            return carry

        lax.fori_loop(0, groups, block, 0)

    def attend(j, h):
        feature = lanes(h * HD, HD)
        tile = rows_all // 2
        k = keys[:, feature]
        lane = lax.broadcasted_iota(jnp.int32, (tile, 128), 1)
        for part in range(2):
            place = slice(part * tile, (part + 1) * tile)
            q = queries[j, place, feature]
            scores = lax.dot_general(q, k, (((1,), (1,)), ((), ())), preferred_element_type=jnp.float32)
            row_max = jnp.max(scores, axis=1, keepdims=True) * SCALE
            weights = jnp.exp2(scores * SCALE - row_max)
            mixed = jnp.dot(weights.astype(jnp.bfloat16), values[h], preferred_element_type=jnp.float32)
            total = mixed[:, HD:]
            partial[j, place, feature] = (mixed[:, :HD] / total).astype(jnp.bfloat16)
            stats_col[place, :] = jnp.where(lane == h, row_max + jnp.log2(total), stats_col[place, :])

    def tables(i, carry):
        video, own_video = video_ref[i], video_ref[rep]
        limit = counts_ref[own_video] * (tokens * 8)
        row, seen = jnp.int32(0), jnp.float32(0.0)
        for b in range(blocks):
            held, own = slot_ref[video, b], slot_ref[own_video, b]
            row += jnp.where(held // rows_held == rep, held % rows_held, 0)
            seen += jnp.where((own // rows_held == i) & (b * tokens < limit), 1.0, 0.0)
        sel_ref[i] = row
        vis_ref[i] = seen
        return carry

    barrier = pltpu.get_barrier_semaphore()
    column = [(wide, ((y + d) % 4) * 4 + z) for d in range(1, 4)]
    peers = [(2 * x + h, y * 4 + (z + d) % 4) for d in range(1, 4) for h in range(2)] + column
    peers += [(2 * x + other, rep)] + [(2 * to + h, rep) for to in (right, left) for h in range(2)]
    for peer in peers:
        pl.semaphore_signal(barrier, inc=1, device_id=peer, device_id_type=MESH)
    loads = [pltpu.make_async_copy(qkv_ref.at[i], qk.at[i], load_sem.at[i]) for i in range(2)]
    loads[0].start()
    start(raw_copies(0))
    loads[1].start()
    start(raw_copies(1))
    loads[0].wait()
    normalize(0)
    pl.semaphore_wait(barrier, len(peers))
    for peer in column:
        pl.semaphore_signal(rows_sem, inc=1, device_id=peer, device_id_type=MESH)
    start(first_copies(0))
    start(first_copies(1))
    lax.fori_loop(0, groups, tables, 0)
    gather(0)
    pl.semaphore_wait(rows_sem, len(column))
    start(cache_copies(0))
    gather(1)
    start(cache_copies(1))
    for h in range(HEADS_CHUNK):
        values[h, 0:quarter, HD:] = jnp.ones((quarter, HD), jnp.bfloat16)

    def shares(owner, carry):
        count = 2 * 24
        here = pl.ds(pl.multiple_of(quarter + owner * count, 16), count)
        filled = jnp.full((count, HD), vis_ref[owner], jnp.float32).astype(jnp.bfloat16)
        for h in range(HEADS_CHUNK):
            values[h, here, HD:] = filled
        return carry

    lax.fori_loop(0, groups, shares, 0)
    stats_col[...] = jnp.zeros_like(stats_col)
    weights_row[...] = jnp.zeros_like(weights_row)
    loads[1].wait()
    normalize(1)

    def spread(j, carry):
        start(own_copies(j))
        start(kv_copies(j))
        return carry

    lax.fori_loop(0, chunks, spread, 0)

    for j in range(2, SLOTS):
        gather(j)
        start(cache_copies(j))
    wait_first(0)
    start(hop_copies(0))
    start(first_copies(2))

    def step(j, carry):
        wait_hop(j)
        wait_kv(j)
        for copy in own_copies(j):
            copy.wait()
        wait_cache(j)
        prepare(j)
        attend(j, 0)

        @pl.when(j + 1 < chunks)
        def _():
            wait_first(j + 1)
            start(hop_copies(j + 1))

        @pl.when(j + 3 < chunks)
        def _():
            start(first_copies(j + 3))

        for early in range(chunks - SLOTS):

            @pl.when(j == early)
            def _():
                for copy in cache_copies(early):
                    copy.wait_send()
                gather(early + SLOTS)
                start(cache_copies(early + SLOTS))

        def rest(h, inner):
            attend(j, h)
            return inner

        lax.fori_loop(1, HEADS_CHUNK, rest, 0)
        for d in range(4):
            stats[j, d] = jnp.transpose(stats_col[d * quarter : (d + 1) * quarter, :])[0:HEADS_CHUNK]
        start(s1_copies(j))

        @pl.when(j >= 1)
        def _():
            forward_partial(j - 1)

        @pl.when(j >= 2)
        def _():
            finish(j - 2)

        return carry

    lax.fori_loop(0, chunks, step, 0)
    forward_partial(chunks - 1)
    finish(chunks - 2)

    def settle(j):
        sent, kept = out_copies(j)
        sent.wait_send()
        sent.wait_recv()
        kept.wait()

    def drain(j, carry):
        @pl.when(j + SLOTS >= chunks)
        def _():
            for copy in cache_copies(j):
                copy.wait_send()

        for copy in first_copies(j) + hop_copies(j) + kv_copies(j) + s1_copies(j):
            copy.wait_send()

        @pl.when(j + 1 < chunks)
        def _():
            for copy in s2_copies(j, 0) + s2_copies(j, 1):
                copy.wait_send()

        @pl.when(j + 2 < chunks)
        def _():
            settle(j)

        return carry

    lax.fori_loop(0, chunks, drain, 0)
    finish(chunks - 1)
    for copy in s2_copies(chunks - 1, 0) + s2_copies(chunks - 1, 1):
        copy.wait_send()
    settle(chunks - 2)
    settle(chunks - 1)


def deliver_kernel(src_ref, dst_ref, held, in_sem, out_sem):
    parts = held.shape[0]
    rows = held.shape[1]
    loads = [pltpu.make_async_copy(src_ref.at[i * rows : (i + 1) * rows], held.at[i], in_sem.at[i]) for i in range(parts)]
    stores = [pltpu.make_async_copy(held.at[i], dst_ref.at[i * rows : (i + 1) * rows], out_sem.at[i]) for i in range(parts)]
    for load in loads:
        load.start()
    for load, store in zip(loads, stores):
        load.wait()
        store.start()
    for store in stores:
        store.wait()


def deliver(array):
    parts = 6
    rows, width = array.shape
    any_spec = pl.BlockSpec(memory_space=pl.ANY)
    return pl.pallas_call(
        deliver_kernel,
        name="deliver",
        out_shape=jax.ShapeDtypeStruct(array.shape, array.dtype),
        in_specs=[any_spec],
        out_specs=any_spec,
        scratch_shapes=[
            pltpu.VMEM((parts, rows // parts, width), array.dtype),
            pltpu.SemaphoreType.DMA((parts,)),
            pltpu.SemaphoreType.DMA((parts,)),
        ],
        compiler_params=pltpu.CompilerParams(vmem_limit_bytes=60 << 20),
    )(array)


def body(stretch_qkv, norm_gains, cache, cached_stretches, block_slot, video_of_group):
    groups = lax.axis_size("rep")
    _, tokens, _, width = stretch_qkv.shape
    slots = cache.shape[0]
    stretch = tokens * lax.axis_size("wide")
    chunks = width // 2 // CHUNK
    bf16, f32 = jnp.bfloat16, jnp.float32
    rows_all = stretch
    quarter = 2 * tokens
    keys_count = quarter + groups * 2 * cache.shape[2]
    vmem, dma = pltpu.VMEM, pltpu.SemaphoreType.DMA
    peers = 2 * len(ORDER) + 1
    smem_spec = pl.BlockSpec(memory_space=pltpu.SMEM)
    any_spec = pl.BlockSpec(memory_space=pl.ANY)
    out = pl.pallas_call(
        kernel,
        name="attend_exchange",
        out_shape=jax.ShapeDtypeStruct((tokens, width), bf16),
        in_specs=[smem_spec, smem_spec, smem_spec, any_spec, pl.BlockSpec(memory_space=vmem), any_spec],
        out_specs=any_spec,
        scratch_shapes=[
            vmem((2, tokens, width), bf16),
            vmem((2, slots, 2, 3, 8, CHUNK), bf16),
            vmem((2, slots, 2, 3, 8, CHUNK), bf16),
            vmem((SLOTS, groups, 2, 2, 3, 8, CHUNK), bf16),
            vmem((chunks, groups, 2, 2, 3, 8, CHUNK), bf16),
            vmem((chunks, rows_all, CHUNK), bf16),
            vmem((chunks, quarter, CHUNK), bf16),
            vmem((chunks, quarter, CHUNK), bf16),
            vmem((keys_count, CHUNK), bf16),
            vmem((HEADS_CHUNK, keys_count, 2 * HD), bf16),
            vmem((chunks, rows_all, CHUNK), bf16),
            vmem((chunks, 2, tokens, CHUNK), bf16),
            vmem((chunks, 2, quarter, CHUNK), bf16),
            vmem((rows_all, 128), f32),
            vmem((chunks, 4, HEADS_CHUNK, quarter), f32),
            vmem((chunks, 2, HEADS_CHUNK, quarter), f32),
            vmem((chunks, 2, HEADS_CHUNK, quarter), f32),
            vmem((128, quarter), f32),
            vmem((quarter, 128), f32),
            pltpu.SMEM((groups,), jnp.int32),
            pltpu.SMEM((groups,), f32),
            dma((2,)),
            dma((2, 2)),
            dma((chunks, 3)),
            dma((chunks, peers)),
            dma((chunks, 2 * groups)),
            dma((chunks, 5)),
            dma((chunks, 5)),
            dma((chunks, 2)),
            dma((chunks, 2)),
            dma((chunks, 2)),
            dma((chunks, 2)),
            dma((chunks, 4)),
            dma((chunks, 4)),
            dma((chunks, 4)),
            dma((chunks, 4)),
            dma((chunks,)),
            dma((chunks,)),
            dma((chunks,)),
            pltpu.SemaphoreType.REGULAR,
        ],
        compiler_params=pltpu.CompilerParams(collective_id=0, has_side_effects=True, vmem_limit_bytes=67043328),
    )(cached_stretches, block_slot, video_of_group, jnp.transpose(stretch_qkv[0], (1, 0, 2)), norm_gains, cache.reshape(slots, 2, 3, 8, width))
    return deliver(out)[None]


def solution(mesh):
    in_specs = (P("rep", "wide", None, None), P(), P("rep", None, "wide", None), P(), P(), P())
    out_specs = P("rep", "wide", None)
    return jax.shard_map(body, mesh=mesh, in_specs=in_specs, out_specs=out_specs, check_vma=False)
```
